32 devices in a mesh: wide: 8 (over z, y), narrow: 4 (over x, core).
Axes of the slice: x: 2, y: 2, z: 4, core: 2. Of those that a mesh axis runs over, the one named last changes fastest.
Arguments:
- activations: bfloat16 [256, 28672], P('wide', 'narrow'), may hold values from -6 to 6
- out_grads: bfloat16 [256, 8192], P('wide'), may hold values from -6 to 6
- basis_in: bfloat16 [28672, 28672], P('narrow', 'wide'), may hold values from -0.03125 to 0.03125
- basis_out: bfloat16 [8192, 8192], P('wide', 'narrow'), may hold values from -0.0625 to 0.0625
- eigenvalues: bfloat16 [8192, 28672], P('narrow', 'wide'), may hold values from 0.29882812 to 10
- queries: bfloat16 [2, 8192, 28672], P(None, 'narrow', 'wide'), may hold values from -0.00036621094 to 0.00036621094
- doc_ids: int32 [256], replicated, may hold values from 0 to 15, never falling along the last dimension, each value on 1 to 32 neighbouring positions
Outputs:
- scores: float32 [16, 2], replicated
The draws below stay inside these ranges and needn't reach their ends.
Inputs may be any that keep to these rules, and one draw needn't show every extreme that they name: `doc_ids`: document numbers never fall along the tokens; each document has 1 to 32 tokens.
All inputs are finite; a program needn't handle non-finite values.
Results may differ from the reference program's by a relative error of at most 0.0051.
Values may be sent and summed in bfloat16 or wider, within the bound.
A program may use at most 192 MiB of HBM per device.

```python
import math
import jax
import jax.numpy as jnp
import numpy as np
from jax import lax

D = 8192
FF = 28672
NQ = 2
TOKENS = 256
DOCS = 16
DOC_MOST = 32


def shard_levels(stream_key, dims, split, smallest, largest):
    level = 1.0
    for position, shards_of in split:
        heights = jax.random.uniform(jax.random.fold_in(jax.random.fold_in(stream_key, 6), position), (shards_of,), jnp.float32, smallest / len(split), largest / len(split))
        level = level * jnp.repeat(jnp.exp(heights), dims[position] // shards_of).reshape((-1,) + (1,) * (len(dims) - 1 - position))
    return level


def profile(number_of, total, bound, skew):
    loads = [(1 << 20) // math.isqrt(standing ** skew) + 1 for standing in range(2, number_of + 1)]
    rest, counts = total - bound - (number_of - 1), [1] * (number_of - 1)
    while rest > 0:
        candidates = [i for i in range(number_of - 1) if counts[i] < bound]
        pool, budget = sum([loads[i] for i in candidates]), rest
        for i in candidates:
            extra = min(bound - counts[i], max(1, budget * loads[i] // pool), rest)
            counts[i] = counts[i] + extra
            rest = rest - extra
    return np.array([bound] + counts)


def uneven(stream_key, number_of, total, bound, slope):
    if number_of == 2:
        one = jax.random.randint(stream_key, (), max(1, total - bound), min(bound, total - 1) + 1)
        return jnp.stack([one, total - one])
    lengths = jnp.asarray(profile(number_of, total, bound, slope), jnp.int32)
    couples = (number_of - 1) // 2
    donor, sink = lengths[1:1 + 2 * couples:2], lengths[2:2 + 2 * couples:2]
    margin = jnp.minimum(donor - 1, bound - sink)
    passed = jax.random.randint(jax.random.fold_in(stream_key, 1), (couples,), 0, 1 << 20) % (margin + 1)
    lengths = lengths.at[1:1 + 2 * couples:2].set(donor - passed).at[2:2 + 2 * couples:2].set(sink + passed)
    return lengths[jax.random.permutation(jax.random.fold_in(stream_key, 2), number_of)]


def centred(stream_key, shape, deviation, most, cuts=(), held_as=jnp.bfloat16):
    factor_of = shard_levels(stream_key, shape, cuts, -0.22, 0.18) if cuts else 1.0
    values = jax.random.normal(stream_key, shape, jnp.float32) * deviation * factor_of
    return jnp.minimum(jnp.maximum(values, -most), most).astype(held_as)


def setup_inputs(seed: int = 0) -> dict:
    keys = jax.random.split(jax.random.key(seed), 8)
    activations = centred(keys[0], (TOKENS, FF), 1.0, 6.0, ((0, 8), (1, 4)))
    out_grads = centred(keys[1], (TOKENS, D), 1.0, 6.0, ((0, 8),))
    basis_in = centred(keys[2], (FF, FF), FF ** -0.5, 0.03125, ((0, 4), (1, 8)))
    basis_out = centred(keys[3], (D, D), D ** -0.5, 0.0625, ((0, 8), (1, 4)))
    eigenvalues = jnp.clip(jnp.exp(math.log(10.0) - 3.5104718 * jax.random.uniform(keys[4], (D, FF), jnp.float32) ** shard_levels(keys[4], (D, FF), ((0, 4), (1, 8)), -0.2, 0.2)), 0.29882812, 10.0).astype(jnp.bfloat16)
    queries = centred(keys[5], (NQ, D, FF), (D * FF) ** -0.5, 0.00036621094, ((1, 4), (2, 8)))
    doc_ids = jnp.searchsorted(jnp.cumsum(uneven(keys[6], DOCS, TOKENS, DOC_MOST, 2)), jnp.arange(TOKENS), side="right").astype(jnp.int32)
    return dict(activations=activations, out_grads=out_grads, basis_in=basis_in, basis_out=basis_out, eigenvalues=eigenvalues, queries=queries, doc_ids=doc_ids)


DAMPING = 0.1


def reference(activations, out_grads, basis_in, basis_out, eigenvalues, queries, doc_ids):
    rot_acts = jnp.dot(activations, basis_in, preferred_element_type=jnp.float32).astype(jnp.bfloat16)
    rot_grads = jnp.dot(out_grads, basis_out, preferred_element_type=jnp.float32).astype(jnp.bfloat16)
    precond = (queries.astype(jnp.float32) / (eigenvalues.astype(jnp.float32)[None] + DAMPING)).astype(jnp.bfloat16)
    acts_float = rot_acts.astype(jnp.float32)

    def per_query(scaled):
        mixed_rows = jnp.dot(rot_grads, scaled, preferred_element_type=jnp.float32)
        return jnp.sum(mixed_rows * acts_float, axis=1)

    token_scores = lax.map(per_query, precond)
    member = (doc_ids[None, :] == jnp.arange(DOCS, dtype=jnp.int32)[:, None]).astype(jnp.float32)
    return jnp.dot(member, token_scores.T, precision=lax.Precision.HIGHEST)
```

```python
import functools

import jax
import jax.numpy as jnp
from jax import lax
from jax.experimental import pallas as pl
from jax.experimental.pallas import tpu as pltpu
from jax.sharding import PartitionSpec as P

DOC_PER = 2
DAMPING = 0.1
F32 = jnp.float32
BF16 = jnp.bfloat16
ANY = pl.BlockSpec(memory_space=pl.ANY)
VMEM_LIMIT = 60 * 1024 * 1024


def tile_of(size, most):
    return max(t for t in range(128, most + 1, 128) if size % t == 0)


def grid_of(wide):
    outer = max(o for o in (1, 2, 3, 4) if wide % o == 0)
    return outer, wide // outer


def remote(src, dst, send, recv, device):
    return pltpu.make_async_remote_copy(
        src_ref=src,
        dst_ref=dst,
        send_sem=send,
        recv_sem=recv,
        device_id=device,
        device_id_type=pl.DeviceIdType.MESH,
    )


def greet(wide, narrow):
    w, n = lax.axis_index("wide"), lax.axis_index("narrow")
    barrier = pltpu.get_barrier_semaphore()
    for d in range(1, wide):
        pl.semaphore_signal(
            barrier, inc=1, device_id={"wide": lax.rem(w + d, wide)}, device_id_type=pl.DeviceIdType.MESH
        )
    for d in range(1, narrow):
        pl.semaphore_signal(
            barrier, inc=1, device_id={"narrow": lax.rem(n + d, narrow)}, device_id_type=pl.DeviceIdType.MESH
        )
    pl.semaphore_wait(barrier, wide + narrow - 2)


def rotate_kernel(
    wide, narrow, acts, grads, basis_in, basis_out, rot_grads, rot_acts,
    acts_all, weights, total, rows_held, weights_out, grads_part, grads_send, first_recv, second_send,
    second_recv, grads_all, acts_send, core_recv, cross_send, cross_recv, acts_done,
    local_sem, weight_sem, out_sem, a2a_s, a2a_r,
    line_s, line_r, side_s, side_r, gline_s, gline_r, gside_s, gside_r,
    first_s, first_r, second_s, second_r, core_s, core_r, cross_s, cross_r, last_s, last_r,
):
    outer, inner = grid_of(wide)
    cross = narrow // 2
    w, n = lax.axis_index("wide"), lax.axis_index("narrow")
    wo, wi = w // inner, lax.rem(w, inner)
    nx, nc = n // 2, lax.rem(n, 2)
    chunks, tokens, depth = acts_all.shape
    block = acts.shape[0]
    columns = total.shape[1]
    rows_out = basis_out.shape[0]
    half = tokens // 2

    def line_peer(d):
        return {"wide": lax.rem(wo + d, outer) * inner + wi}

    def side_peer(e):
        return {"wide": wo * inner + lax.rem(wi + e, inner)}

    def cut(c):
        return pl.ds(pl.multiple_of(c * depth, 128), depth)

    def rows(source):
        return pl.ds(pl.multiple_of(source * block, block), block)

    def line_source(d):
        return lax.rem(wo + outer - d, outer) * inner + wi

    def weight(c):
        slot = lax.rem(c, 2)
        return pltpu.make_async_copy(
            basis_in.at[pl.ds(pl.multiple_of(c * depth, 128), depth)], weights.at[slot], weight_sem.at[slot]
        )

    fetch_out = pltpu.make_async_copy(basis_out, weights_out, local_sem.at[0])
    own_rows = pltpu.make_async_copy(
        grads.at[:, pl.ds(pl.multiple_of(w * rows_out, 128), rows_out)], rows_held.at[rows(w)], local_sem.at[1]
    )

    def own_acts(c):
        return pltpu.make_async_copy(acts.at[:, cut(c)], acts_all.at[c, rows(w)], out_sem.at[c])

    own_rows.start()
    fetch_out.start()
    for c in range(chunks):
        own_acts(c).start()
    weight(0).start()
    weight(1).start()
    greet(wide, narrow)

    def swap(d):
        to = lax.rem(w + d, wide)
        return remote(
            grads.at[:, pl.ds(pl.multiple_of(to * rows_out, 128), rows_out)],
            rows_held.at[rows(w)],
            a2a_s.at[d],
            a2a_r.at[d],
            {"wide": to},
        )

    for d in range(1, wide):
        swap(d).start()

    def line_copy(c, d):
        return remote(
            acts.at[:, cut(c)], acts_all.at[c, rows(w)], line_s.at[c, d], line_r.at[c, d], line_peer(d)
        )

    def side_own(c, e):
        return remote(
            acts.at[:, cut(c)], acts_all.at[c, rows(w)], side_s.at[c, e, 0], side_r.at[c, e, 0], side_peer(e)
        )

    def side_pass(c, e, d):
        source = line_source(d)
        return remote(
            acts_all.at[c, rows(source)],
            acts_all.at[c, rows(source)],
            side_s.at[c, e, d],
            side_r.at[c, e, d],
            side_peer(e),
        )

    def begin(c, carry):
        for d in range(1, outer):
            line_copy(c, d).start()
        for e in range(1, inner):
            side_own(c, e).start()
        return carry

    lax.fori_loop(0, chunks, begin, 0)

    own_rows.wait()
    fetch_out.wait()
    for d in range(1, wide):
        swap(d).wait_recv()
    width = weights_out.shape[1]
    wt = tile_of(width, 512)

    def grads_tile(k, carry):
        at = pl.ds(pl.multiple_of(k * wt, 128), wt)
        part = jnp.dot(rows_held[...], weights_out[:, at], preferred_element_type=F32)
        part = part.reshape(outer, inner, block, wt)
        grads_part[:, :, :, at] = part
        grads_send[:, :, :, at] = part.astype(BF16)
        return carry

    lax.fori_loop(0, width // wt, grads_tile, 0)

    def first(e):
        return remote(
            grads_send.at[:, lax.rem(wi + e, inner)], first_recv.at[e], first_s.at[e], first_r.at[e], side_peer(e)
        )

    for e in range(1, inner):
        first(e).start()

    def second(d):
        return remote(
            second_send.at[lax.rem(wo + d, outer)], second_recv.at[d], second_s.at[d], second_r.at[d], line_peer(d)
        )

    ct = tile_of(columns, 512)

    def forward(c):
        for d in range(1, outer):
            line_copy(c, d).wait_recv()
            for e in range(1, inner):
                side_pass(c, e, d).start()

    def step(c, carry):
        @pl.when(c + 1 < chunks)
        def _():
            forward(c + 1)

        own_acts(c).wait()
        for e in range(1, inner):
            side_own(c, e).wait_recv()
            for d in range(1, outer):
                side_pass(c, e, d).wait_recv()
        weight(c).wait()
        slot = lax.rem(c, 2)

        def tile(k, carry):
            at = pl.ds(pl.multiple_of(k * ct, 128), ct)
            part = jnp.dot(acts_all[c], weights[slot, :, at], preferred_element_type=F32)

            @pl.when(c == 0)
            def _():
                total[:, at] = part

            @pl.when(c > 0)
            def _():
                total[:, at] += part

            return carry

        lax.fori_loop(0, columns // ct, tile, 0)

        @pl.when(c + 2 < chunks)
        def _():
            weight(c + 2).start()

        return carry

    middle = chunks // 2
    forward(0)
    lax.fori_loop(0, middle, step, 0)
    for e in range(1, inner):
        first(e).wait_recv()
    for o in range(outer):
        value = grads_part[o, wi]
        for e in range(1, inner):
            value = value + first_recv[e, o].astype(F32)
        grads_part[o, wi] = value
        second_send[o] = value.astype(BF16)
    for d in range(1, outer):
        second(d).start()
    lax.fori_loop(middle, chunks, step, 0)

    def to_send(k, carry):
        at = pl.ds(pl.multiple_of(k * ct, 128), ct)
        acts_send[:, at] = total[pl.ds(pl.multiple_of((1 - nc) * half, half), half), at].astype(BF16)
        return carry

    lax.fori_loop(0, columns // ct, to_send, 0)
    partner = {"narrow": nx * 2 + (1 - nc)}
    core_copy = remote(acts_send, core_recv, core_s, core_r, partner)
    core_copy.start()

    for d in range(1, outer):
        second(d).wait_recv()
    value = grads_part[wo, wi]
    for d in range(1, outer):
        value = value + second_recv[d].astype(F32)
    grads_all[w] = value.astype(BF16)

    def gline(d):
        return remote(grads_all.at[w], grads_all.at[w], gline_s.at[d], gline_r.at[d], line_peer(d))

    def gside(e, d):
        source = line_source(d)
        return remote(
            grads_all.at[source], grads_all.at[source], gside_s.at[e, d], gside_r.at[e, d], side_peer(e)
        )

    for d in range(1, outer):
        gline(d).start()
    for e in range(1, inner):
        gside(e, 0).start()

    mine = pl.ds(pl.multiple_of(nc * half, half), half)
    core_copy.wait_recv()

    def core_sum(k, carry):
        at = pl.ds(pl.multiple_of(k * ct, 128), ct)
        value = total[mine, at] + core_recv[:, at].astype(F32)
        total[mine, at] = value
        cross_send[:, at] = value.astype(BF16)
        return carry

    lax.fori_loop(0, columns // ct, core_sum, 0)

    def cross_copy(d):
        return remote(
            cross_send, cross_recv.at[d], cross_s.at[d], cross_r.at[d], {"narrow": lax.rem(nx + d, cross) * 2 + nc}
        )

    for d in range(1, cross):
        cross_copy(d).start()
    for d in range(1, outer):
        gline(d).wait_recv()
        for e in range(1, inner):
            gside(e, d).start()
    for d in range(1, cross):
        cross_copy(d).wait_recv()

    def cross_sum(k, carry):
        at = pl.ds(pl.multiple_of(k * ct, 128), ct)
        value = total[mine, at]
        for d in range(1, cross):
            value = value + cross_recv[d, :, at].astype(F32)
        acts_done[nc, :, at] = value.astype(BF16)
        return carry

    lax.fori_loop(0, columns // ct, cross_sum, 0)
    last = remote(acts_done.at[nc], acts_done.at[nc], last_s, last_r, partner)
    last.start()
    for e in range(1, inner):
        for d in range(outer):
            gside(e, d).wait_recv()
    put_grads = pltpu.make_async_copy(grads_all, rot_grads, local_sem.at[0])
    put_grads.start()
    last.wait_recv()
    put_acts = pltpu.make_async_copy(acts_done, rot_acts, local_sem.at[1])
    put_acts.start()

    for d in range(1, wide):
        swap(d).wait_send()

    def drain(c, carry):
        for d in range(1, outer):
            line_copy(c, d).wait_send()
        for e in range(1, inner):
            side_own(c, e).wait_send()
            for d in range(1, outer):
                side_pass(c, e, d).wait_send()
        return carry

    lax.fori_loop(0, chunks, drain, 0)
    for e in range(1, inner):
        first(e).wait_send()
        for d in range(outer):
            gside(e, d).wait_send()
    for d in range(1, outer):
        second(d).wait_send()
        gline(d).wait_send()
    core_copy.wait_send()
    for d in range(1, cross):
        cross_copy(d).wait_send()
    last.wait_send()
    put_grads.wait()
    put_acts.wait()


def rotate(wide, narrow, activations, out_grads, basis_in, basis_out):
    outer, inner = grid_of(wide)
    cross = narrow // 2
    block, depth_all = activations.shape
    tokens = block * wide
    depth = tile_of(depth_all, 1024)
    chunks = depth_all // depth
    columns = basis_in.shape[1]
    rows_out, width = basis_out.shape
    half = tokens // 2
    dma = pltpu.SemaphoreType.DMA
    grads, acts = pl.pallas_call(
        functools.partial(rotate_kernel, wide, narrow),
        out_shape=(
            jax.ShapeDtypeStruct((wide, block, width), BF16),
            jax.ShapeDtypeStruct((2, half, columns), BF16),
        ),
        in_specs=[ANY] * 4,
        out_specs=(ANY, ANY),
        scratch_shapes=[
            pltpu.VMEM((chunks, tokens, depth), BF16),
            pltpu.VMEM((2, depth, columns), BF16),
            pltpu.VMEM((tokens, columns), F32),
            pltpu.VMEM((tokens, rows_out), BF16),
            pltpu.VMEM((rows_out, width), BF16),
            pltpu.VMEM((outer, inner, block, width), F32),
            pltpu.VMEM((outer, inner, block, width), BF16),
            pltpu.VMEM((inner, outer, block, width), BF16),
            pltpu.VMEM((outer, block, width), BF16),
            pltpu.VMEM((outer, block, width), BF16),
            pltpu.VMEM((wide, block, width), BF16),
            pltpu.VMEM((half, columns), BF16),
            pltpu.VMEM((half, columns), BF16),
            pltpu.VMEM((half, columns), BF16),
            pltpu.VMEM((cross, half, columns), BF16),
            pltpu.VMEM((2, half, columns), BF16),
            dma((2,)),
            dma((2,)),
            dma((chunks,)),
            dma((wide,)),
            dma((wide,)),
            dma((chunks, outer)),
            dma((chunks, outer)),
            dma((chunks, inner, outer)),
            dma((chunks, inner, outer)),
            dma((outer,)),
            dma((outer,)),
            dma((inner, outer)),
            dma((inner, outer)),
            dma((inner,)),
            dma((inner,)),
            dma((outer,)),
            dma((outer,)),
            dma,
            dma,
            dma((cross,)),
            dma((cross,)),
            dma,
            dma,
        ],
        compiler_params=pltpu.CompilerParams(
            collective_id=0, has_side_effects=True, vmem_limit_bytes=VMEM_LIMIT
        ),
        name="rotate",
    )(activations, out_grads, basis_in, basis_out)
    return grads.reshape(tokens, width), acts.reshape(tokens, columns)


def mix_kernel(docs, grads, acts, eigenvalues, queries, ids, out, lanes):
    j = pl.program_id(0)

    @pl.when(j == 0)
    def _():
        lanes[...] = jnp.zeros_like(lanes)

    scale = 1.0 / (eigenvalues[...].astype(F32) + DAMPING)
    acts_float = acts[...].astype(F32)
    for q in range(queries.shape[0]):
        precond = (queries[q].astype(F32) * scale).astype(BF16)
        mixed = jnp.dot(grads[...], precond, preferred_element_type=F32) * acts_float
        part = mixed[:, :128]
        for k in range(1, mixed.shape[1] // 128):
            part = part + mixed[:, k * 128 : (k + 1) * 128]
        lanes[q] += part

    @pl.when(j == pl.num_programs(0) - 1)
    def _():
        tokens = lanes.shape[1]
        member = (ids[...] == lax.broadcasted_iota(jnp.int32, (docs, tokens), 0)).astype(F32)
        for q in range(queries.shape[0]):
            out[q] = jnp.dot(member, lanes[q], precision=lax.Precision.HIGHEST, preferred_element_type=F32)


def mix(docs, rot_grads, rot_acts, eigenvalues, queries, doc_ids):
    tokens, width = rot_grads.shape
    count, _, columns = queries.shape
    tile = tile_of(columns, 256)
    return pl.pallas_call(
        functools.partial(mix_kernel, docs),
        grid=(columns // tile,),
        out_shape=jax.ShapeDtypeStruct((count, docs, 128), F32),
        in_specs=[
            pl.BlockSpec((tokens, width), lambda j: (0, 0)),
            pl.BlockSpec((tokens, tile), lambda j: (0, j)),
            pl.BlockSpec((width, tile), lambda j: (0, j)),
            pl.BlockSpec((count, width, tile), lambda j: (0, 0, j)),
            pl.BlockSpec((1, tokens), lambda j: (0, 0)),
        ],
        out_specs=pl.BlockSpec((count, docs, 128), lambda j: (0, 0, 0)),
        scratch_shapes=[pltpu.VMEM((count, tokens, 128), F32)],
        compiler_params=pltpu.CompilerParams(vmem_limit_bytes=VMEM_LIMIT),
        name="mix",
    )(rot_grads, rot_acts, eigenvalues, queries, doc_ids.reshape(1, tokens))


def add_kernel(wide, narrow, part, out, held, across, send_w, recv_w, send_n, recv_n):
    w, n = lax.axis_index("wide"), lax.axis_index("narrow")
    greet(wide, narrow)

    def over_narrow(d):
        return remote(
            part, across.at[n], send_n.at[d], recv_n.at[d], {"narrow": lax.rem(n + d, narrow)}
        )

    def over_wide(d):
        return remote(
            held.at[w], held.at[w], send_w.at[d], recv_w.at[d], {"wide": lax.rem(w + d, wide)}
        )

    for d in range(1, narrow):
        over_narrow(d).start()
    across[n] = part[...]
    for d in range(1, narrow):
        over_narrow(d).wait_recv()
    value = across[0]
    for d in range(1, narrow):
        value = value + across[d]
    held[w] = value
    for d in range(1, wide):
        over_wide(d).start()
    for d in range(1, wide):
        over_wide(d).wait_recv()
    value = held[0]
    for d in range(1, wide):
        value = value + held[d]
    sums = jnp.sum(value, axis=2)
    for q in range(part.shape[0]):
        out[q : q + 1, :] = sums[q : q + 1, :]
    for d in range(1, narrow):
        over_narrow(d).wait_send()
    for d in range(1, wide):
        over_wide(d).wait_send()


def add_up(wide, narrow, part):
    dma = pltpu.SemaphoreType.DMA
    return pl.pallas_call(
        functools.partial(add_kernel, wide, narrow),
        out_shape=jax.ShapeDtypeStruct(part.shape[:2], F32),
        in_specs=[pl.BlockSpec(memory_space=pltpu.VMEM)],
        out_specs=pl.BlockSpec(memory_space=pltpu.VMEM),
        scratch_shapes=[
            pltpu.VMEM((wide,) + part.shape, F32),
            pltpu.VMEM((narrow,) + part.shape, F32),
            dma((wide,)),
            dma((wide,)),
            dma((narrow,)),
            dma((narrow,)),
        ],
        compiler_params=pltpu.CompilerParams(collective_id=1, has_side_effects=True),
        name="add_up",
    )(part)


def solution(mesh):
    wide, narrow = mesh.shape["wide"], mesh.shape["narrow"]

    def shards(activations, out_grads, basis_in, basis_out, eigenvalues, queries, doc_ids):
        rot_grads, rot_acts = rotate(wide, narrow, activations, out_grads, basis_in, basis_out)
        part = mix(DOC_PER * wide, rot_grads, rot_acts, eigenvalues, queries, doc_ids)
        return add_up(wide, narrow, part).T

    return jax.shard_map(
        shards,
        mesh=mesh,
        in_specs=(
            P("wide", "narrow"),
            P("wide", None),
            P("narrow", "wide"),
            P("wide", "narrow"),
            P("narrow", "wide"),
            P(None, "narrow", "wide"),
            P(),
        ),
        out_specs=P(),
        check_vma=False,
    )
```

```python
import functools

import jax
import jax.numpy as jnp
from jax import lax
from jax.experimental import pallas as pl
from jax.experimental.pallas import tpu as pltpu
from jax.sharding import PartitionSpec as P

DOC_PER = 2
DAMPING = 0.1
F32 = jnp.float32
BF16 = jnp.bfloat16
ANY = pl.BlockSpec(memory_space=pl.ANY)
VMEM_LIMIT = 67_043_328


def tile_of(size, most):
    return max(t for t in range(128, most + 1, 128) if size % t == 0)


def grid_of(wide):
    outer = max(o for o in (1, 2, 3, 4) if wide % o == 0)
    return outer, wide // outer


def remote(src, dst, send, recv, device):
    return pltpu.make_async_remote_copy(
        src_ref=src,
        dst_ref=dst,
        send_sem=send,
        recv_sem=recv,
        device_id=device,
        device_id_type=pl.DeviceIdType.MESH,
    )


def greet(wide, narrow):
    w, n = lax.axis_index("wide"), lax.axis_index("narrow")
    barrier = pltpu.get_barrier_semaphore()
    for d in range(1, wide):
        pl.semaphore_signal(
            barrier, inc=1, device_id={"wide": lax.rem(w + d, wide)}, device_id_type=pl.DeviceIdType.MESH
        )
    for d in range(1, narrow):
        pl.semaphore_signal(
            barrier, inc=1, device_id={"narrow": lax.rem(n + d, narrow)}, device_id_type=pl.DeviceIdType.MESH
        )
    pl.semaphore_wait(barrier, wide + narrow - 2)


def score_kernel(
    wide, narrow, docs, acts, grads, basis_in, basis_out, eigenvalues, queries, ids, out, precond,
    acts_all, weights, total, rows_held, weights_out, grads_part, grads_send, first_recv, second_send,
    second_recv, grads_all, acts_send, core_recv, cross_send, cross_recv, acts_done,
    eig_tile, query_tile, pre_tile, mix_tile, mixed, lanes, held, across,
    local_sem, weight_sem, out_sem, eig_sem, query_sem, put_sem, get_sem, a2a_s, a2a_r,
    line_s, line_r, side_s, side_r, gline_s, gline_r, gside_s, gside_r,
    first_s, first_r, second_s, second_r, core_s, core_r, cross_s, cross_r, done_s, done_r, last_s, last_r,
    send_w, recv_w, send_n, recv_n,
):
    outer, inner = grid_of(wide)
    cross = narrow // 2
    w, n = lax.axis_index("wide"), lax.axis_index("narrow")
    wo, wi = w // inner, lax.rem(w, inner)
    nx, nc = n // 2, lax.rem(n, 2)
    chunks, tokens, depth = acts_all.shape
    block = acts.shape[0]
    columns = total.shape[1]
    rows_out = basis_out.shape[0]
    half = tokens // 2

    def line_peer(d):
        return {"wide": lax.rem(wo + d, outer) * inner + wi}

    def side_peer(e):
        return {"wide": wo * inner + lax.rem(wi + e, inner)}

    def cut(c):
        return pl.ds(pl.multiple_of(c * depth, 128), depth)

    def rows(source):
        return pl.ds(pl.multiple_of(source * block, block), block)

    def line_source(d):
        return lax.rem(wo + outer - d, outer) * inner + wi

    def weight(c):
        slot = lax.rem(c, 2)
        return pltpu.make_async_copy(
            basis_in.at[pl.ds(pl.multiple_of(c * depth, 128), depth)], weights.at[slot], weight_sem.at[slot]
        )

    fetch_out = pltpu.make_async_copy(basis_out, weights_out, local_sem.at[0])
    own_rows = pltpu.make_async_copy(
        grads.at[:, pl.ds(pl.multiple_of(w * rows_out, 128), rows_out)], rows_held.at[rows(w)], local_sem.at[1]
    )

    def own_acts(c):
        return pltpu.make_async_copy(acts.at[:, cut(c)], acts_all.at[c, rows(w)], out_sem.at[c])

    own_rows.start()
    fetch_out.start()
    for c in range(chunks):
        own_acts(c).start()
    weight(0).start()
    weight(1).start()
    count, width, _ = queries.shape
    slab = eig_tile.shape[1]
    slabs = width // slab

    def slab_rows(k):
        return pl.ds(pl.multiple_of(k * slab, 16), slab)

    def eig_copy(k):
        slot = lax.rem(k, 2)
        return pltpu.make_async_copy(eigenvalues.at[slab_rows(k)], eig_tile.at[slot], eig_sem.at[slot])

    def query_copy(k):
        slot = lax.rem(k, 2)
        return pltpu.make_async_copy(queries.at[:, slab_rows(k)], query_tile.at[slot], query_sem.at[slot])

    def put_copy(k):
        slot = lax.rem(k, 2)
        return pltpu.make_async_copy(pre_tile.at[slot], precond.at[:, slab_rows(k)], put_sem.at[slot])

    for k in range(2):
        eig_copy(k).start()
        query_copy(k).start()
    greet(wide, narrow)

    def swap(d):
        to = lax.rem(w + d, wide)
        return remote(
            grads.at[:, pl.ds(pl.multiple_of(to * rows_out, 128), rows_out)],
            rows_held.at[rows(w)],
            a2a_s.at[d],
            a2a_r.at[d],
            {"wide": to},
        )

    def line_copy(c, d):
        return remote(
            acts.at[:, cut(c)], acts_all.at[c, rows(w)], line_s.at[c, d], line_r.at[c, d], line_peer(d)
        )

    def side_own(c, e):
        return remote(
            acts.at[:, cut(c)], acts_all.at[c, rows(w)], side_s.at[c, e, 0], side_r.at[c, e, 0], side_peer(e)
        )

    def side_pass(c, e, d):
        source = line_source(d)
        return remote(
            acts_all.at[c, rows(source)],
            acts_all.at[c, rows(source)],
            side_s.at[c, e, d],
            side_r.at[c, e, d],
            side_peer(e),
        )

    def begin(c, carry):
        for d in range(1, outer):
            line_copy(c, d).start()
        for e in range(1, inner):
            side_own(c, e).start()
        return carry

    early = (chunks + 1) // 3
    middle = (2 * chunks) // 3
    lax.fori_loop(0, early, begin, 0)
    for d in range(1, wide):
        swap(d).start()
    lax.fori_loop(early, chunks, begin, 0)
    wt = tile_of(width, 512)

    def grads_tile(k, carry):
        at = pl.ds(pl.multiple_of(k * wt, 128), wt)
        part = jnp.dot(rows_held[...], weights_out[:, at], preferred_element_type=F32)
        part = part.reshape(outer, inner, block, wt)
        grads_part[:, :, :, at] = part
        grads_send[:, :, :, at] = part.astype(BF16)
        return carry

    def first(e):
        return remote(
            grads_send.at[:, lax.rem(wi + e, inner)], first_recv.at[e], first_s.at[e], first_r.at[e], side_peer(e)
        )

    def second(d):
        return remote(
            second_send.at[lax.rem(wo + d, outer)], second_recv.at[d], second_s.at[d], second_r.at[d], line_peer(d)
        )

    ct = tile_of(columns, 512)

    def forward(c):
        for d in range(1, outer):
            line_copy(c, d).wait_recv()
            for e in range(1, inner):
                side_pass(c, e, d).start()

    ps = tile_of(columns, 512)

    def condition(k):
        slot = lax.rem(k, 2)
        eig_copy(k).wait()
        query_copy(k).wait()

        @pl.when(k >= 2)
        def _():
            put_copy(k - 2).wait()

        def piece(m, carry):
            at = pl.ds(pl.multiple_of(m * ps, 128), ps)
            scale = 1.0 / (eig_tile[slot, :, at].astype(F32) + DAMPING)
            for q in range(count):
                pre_tile[slot, q, :, at] = (query_tile[slot, q, :, at].astype(F32) * scale).astype(BF16)
            return carry

        lax.fori_loop(0, columns // ps, piece, 0)
        put_copy(k).start()

        @pl.when(k + 2 < slabs)
        def _():
            eig_copy(k + 2).start()
            query_copy(k + 2).start()

    each = pl.cdiv(slabs, chunks)

    def step(c, carry):
        def slab_step(m, inside):
            @pl.when(c * each + m < slabs)
            def _():
                condition(c * each + m)

            return inside

        @pl.when(c + 1 < chunks)
        def _():
            forward(c + 1)

        own_acts(c).wait()
        for e in range(1, inner):
            side_own(c, e).wait_recv()
            for d in range(1, outer):
                side_pass(c, e, d).wait_recv()
        weight(c).wait()
        slot = lax.rem(c, 2)

        def tile(k, carry):
            at = pl.ds(pl.multiple_of(k * ct, 128), ct)
            part = jnp.dot(acts_all[c], weights[slot, :, at], preferred_element_type=F32)

            @pl.when(c == 0)
            def _():
                total[:, at] = part

            @pl.when(c > 0)
            def _():
                total[:, at] += part

            return carry

        lax.fori_loop(0, columns // ct, tile, 0)

        @pl.when(c + 2 < chunks)
        def _():
            weight(c + 2).start()

        lax.fori_loop(0, each, slab_step, 0)

        return carry

    forward(0)
    lax.fori_loop(0, early, step, 0)
    own_rows.wait()
    fetch_out.wait()
    for d in range(1, wide):
        swap(d).wait_recv()
    lax.fori_loop(0, width // wt, grads_tile, 0)
    for e in range(1, inner):
        first(e).start()
    lax.fori_loop(early, middle, step, 0)
    for e in range(1, inner):
        first(e).wait_recv()
    for o in range(outer):
        value = grads_part[o, wi]
        for e in range(1, inner):
            value = value + first_recv[e, o].astype(F32)
        second_send[o] = value
    for d in range(1, outer):
        second(d).start()
    lax.fori_loop(middle, chunks, step, 0)

    share = half // cross

    def to_send(k, carry):
        at = pl.ds(pl.multiple_of(k * ct, 128), ct)
        acts_send[:, at] = total[pl.ds(pl.multiple_of((1 - nc) * half, half), half), at]
        return carry

    lax.fori_loop(0, columns // ct, to_send, 0)
    partner = {"narrow": nx * 2 + (1 - nc)}

    def cross_peer(d):
        return {"narrow": lax.rem(nx + d, cross) * 2 + nc}

    core_copy = remote(acts_send, core_recv, core_s, core_r, partner)
    core_copy.start()

    for k in range(min(2, slabs)):
        put_copy(slabs - 1 - k).wait()
    jt = mix_tile.shape[3]
    tiles = columns // jt

    def get_copy(j):
        slot = lax.rem(j, 2)
        return pltpu.make_async_copy(
            precond.at[:, :, pl.ds(pl.multiple_of(j * jt, 128), jt)], mix_tile.at[slot], get_sem.at[slot]
        )

    for j in range(2):
        get_copy(j).start()

    core_copy.wait_recv()

    def core_sum(k, carry):
        at = pl.ds(pl.multiple_of(k * ct, 128), ct)
        value = total[pl.ds(pl.multiple_of(nc * half, half), half), at] + core_recv[:, at]
        for x in range(cross):
            cross_send[x, :, at] = value[x * share : (x + 1) * share]
        return carry

    lax.fori_loop(0, columns // ct, core_sum, 0)

    def cross_copy(d):
        return remote(
            cross_send.at[lax.rem(nx + d, cross)], cross_recv.at[d], cross_s.at[d], cross_r.at[d], cross_peer(d)
        )

    for d in range(1, cross):
        cross_copy(d).start()

    for d in range(1, outer):
        second(d).wait_recv()
    value = second_send[wo]
    for d in range(1, outer):
        value = value + second_recv[d]
    grads_all[w] = value.astype(BF16)

    def gline(d):
        return remote(grads_all.at[w], grads_all.at[w], gline_s.at[d], gline_r.at[d], line_peer(d))

    def gside(e, d):
        source = line_source(d)
        return remote(
            grads_all.at[source], grads_all.at[source], gside_s.at[e, d], gside_r.at[e, d], side_peer(e)
        )

    for d in range(1, outer):
        gline(d).start()
    for e in range(1, inner):
        gside(e, 0).start()
    for d in range(1, outer):
        gline(d).wait_recv()
        for e in range(1, inner):
            gside(e, d).start()
    for e in range(1, inner):
        for d in range(outer):
            gside(e, d).wait_recv()

    def mix(j, carry):
        slot = lax.rem(j, 2)
        get_copy(j).wait()
        left = grads_all[...].reshape(tokens, width)
        at = pl.ds(pl.multiple_of(j * jt, 128), jt)
        for q in range(count):
            mixed[q, :, at] = jnp.dot(left, mix_tile[slot, q], preferred_element_type=F32)

        @pl.when(j + 2 < tiles)
        def _():
            get_copy(j + 2).start()

        return carry

    first_part = tiles // 4
    second_part = (3 * tiles) // 4
    lax.fori_loop(0, first_part, mix, 0)
    for d in range(1, cross):
        cross_copy(d).wait_recv()

    def cross_sum(k, carry):
        at = pl.ds(pl.multiple_of(k * ct, 128), ct)
        value = cross_send[nx, :, at]
        for d in range(1, cross):
            value = value + cross_recv[d, :, at]
        acts_done[nc, nx, :, at] = value.astype(BF16)
        return carry

    lax.fori_loop(0, columns // ct, cross_sum, 0)

    def done_copy(d):
        return remote(acts_done.at[nc, nx], acts_done.at[nc, nx], done_s.at[d], done_r.at[d], cross_peer(d))

    def last_copy(d):
        x = lax.rem(nx + cross - d, cross)
        return remote(acts_done.at[nc, x], acts_done.at[nc, x], last_s.at[d], last_r.at[d], partner)

    for d in range(1, cross):
        done_copy(d).start()
    last_copy(0).start()
    lax.fori_loop(first_part, second_part, mix, 0)
    for d in range(1, cross):
        done_copy(d).wait_recv()
        last_copy(d).start()
    lax.fori_loop(second_part, tiles, mix, 0)
    for d in range(cross):
        last_copy(d).wait_recv()

    lanes[...] = jnp.zeros_like(lanes)

    def fold(j, carry):
        at = pl.ds(pl.multiple_of(j * 128, 128), 128)
        right = acts_done[:, :, :, at].reshape(tokens, 128).astype(F32)
        for q in range(count):
            lanes[q] += mixed[q, :, at] * right
        return carry

    lax.fori_loop(0, columns // 128, fold, 0)
    _, rows_pad, docs_pad = across.shape
    member = (ids[...] == lax.broadcasted_iota(jnp.int32, (docs_pad, tokens), 0)).astype(F32)
    row = lax.broadcasted_iota(jnp.int32, (rows_pad, docs_pad), 0)
    value = jnp.zeros((rows_pad, docs_pad), F32)
    for q in range(count):
        doc_lanes = jnp.dot(member, lanes[q], precision=lax.Precision.HIGHEST, preferred_element_type=F32)
        value = jnp.where(row == q, jnp.sum(doc_lanes, axis=1)[None, :], value)
    across[n] = value

    def over_narrow(d):
        return remote(across.at[n], across.at[n], send_n.at[d], recv_n.at[d], {"narrow": lax.rem(n + d, narrow)})

    def over_wide(d):
        return remote(held.at[w], held.at[w], send_w.at[d], recv_w.at[d], {"wide": lax.rem(w + d, wide)})

    for d in range(1, narrow):
        over_narrow(d).start()
    for d in range(1, narrow):
        over_narrow(d).wait_recv()
    value = across[0]
    for d in range(1, narrow):
        value = value + across[d]
    held[w] = value
    for d in range(1, wide):
        over_wide(d).start()
    for d in range(1, wide):
        over_wide(d).wait_recv()
    value = held[0]
    for d in range(1, wide):
        value = value + held[d]
    out[...] = value[: out.shape[0], : out.shape[1]]

    for d in range(1, wide):
        swap(d).wait_send()

    def drain(c, carry):
        for d in range(1, outer):
            line_copy(c, d).wait_send()
        for e in range(1, inner):
            side_own(c, e).wait_send()
            for d in range(1, outer):
                side_pass(c, e, d).wait_send()
        return carry

    lax.fori_loop(0, chunks, drain, 0)
    for e in range(1, inner):
        first(e).wait_send()
        for d in range(outer):
            gside(e, d).wait_send()
    for d in range(1, outer):
        second(d).wait_send()
        gline(d).wait_send()
    core_copy.wait_send()
    for d in range(1, cross):
        cross_copy(d).wait_send()
        done_copy(d).wait_send()
    for d in range(cross):
        last_copy(d).wait_send()
    for d in range(1, narrow):
        over_narrow(d).wait_send()
    for d in range(1, wide):
        over_wide(d).wait_send()


def score(wide, narrow, activations, out_grads, basis_in, basis_out, eigenvalues, queries, doc_ids):
    outer, inner = grid_of(wide)
    cross = narrow // 2
    block, depth_all = activations.shape
    tokens = block * wide
    docs = DOC_PER * wide
    depth = tile_of(depth_all, 1024)
    chunks = depth_all // depth
    columns = basis_in.shape[1]
    rows_out, width = basis_out.shape
    count = queries.shape[0]
    half = tokens // 2
    slab = tile_of(width, 128) // 2
    jt = tile_of(columns, 256)
    rows_pad, docs_pad = pl.cdiv(count, 8) * 8, pl.cdiv(docs, 128) * 128
    dma = pltpu.SemaphoreType.DMA
    scores, _ = pl.pallas_call(
        functools.partial(score_kernel, wide, narrow, docs),
        out_shape=(
            jax.ShapeDtypeStruct((count, docs), F32),
            jax.ShapeDtypeStruct((count, width, columns), BF16),
        ),
        in_specs=[ANY] * 6 + [pl.BlockSpec(memory_space=pltpu.VMEM)],
        out_specs=(pl.BlockSpec(memory_space=pltpu.VMEM), ANY),
        scratch_shapes=[
            pltpu.VMEM((chunks, tokens, depth), BF16),
            pltpu.VMEM((2, depth, columns), BF16),
            pltpu.VMEM((tokens, columns), F32),
            pltpu.VMEM((tokens, rows_out), BF16),
            pltpu.VMEM((rows_out, width), BF16),
            pltpu.VMEM((outer, inner, block, width), F32),
            pltpu.VMEM((outer, inner, block, width), BF16),
            pltpu.VMEM((inner, outer, block, width), BF16),
            pltpu.VMEM((outer, block, width), F32),
            pltpu.VMEM((outer, block, width), F32),
            pltpu.VMEM((wide, block, width), BF16),
            pltpu.VMEM((half, columns), F32),
            pltpu.VMEM((half, columns), F32),
            pltpu.VMEM((cross, half // cross, columns), F32),
            pltpu.VMEM((cross, half // cross, columns), F32),
            pltpu.VMEM((2, cross, half // cross, columns), BF16),
            pltpu.VMEM((2, slab, columns), BF16),
            pltpu.VMEM((2, count, slab, columns), BF16),
            pltpu.VMEM((2, count, slab, columns), BF16),
            pltpu.VMEM((2, count, width, jt), BF16),
            pltpu.VMEM((count, tokens, columns), F32),
            pltpu.VMEM((count, tokens, 128), F32),
            pltpu.VMEM((wide, rows_pad, docs_pad), F32),
            pltpu.VMEM((narrow, rows_pad, docs_pad), F32),
            dma((2,)),
            dma((2,)),
            dma((chunks,)),
            dma((2,)),
            dma((2,)),
            dma((2,)),
            dma((2,)),
            dma((wide,)),
            dma((wide,)),
            dma((chunks, outer)),
            dma((chunks, outer)),
            dma((chunks, inner, outer)),
            dma((chunks, inner, outer)),
            dma((outer,)),
            dma((outer,)),
            dma((inner, outer)),
            dma((inner, outer)),
            dma((inner,)),
            dma((inner,)),
            dma((outer,)),
            dma((outer,)),
            dma,
            dma,
            dma((cross,)),
            dma((cross,)),
            dma((cross,)),
            dma((cross,)),
            dma((cross,)),
            dma((cross,)),
            dma((wide,)),
            dma((wide,)),
            dma((narrow,)),
            dma((narrow,)),
        ],
        compiler_params=pltpu.CompilerParams(
            collective_id=0, has_side_effects=True, vmem_limit_bytes=VMEM_LIMIT
        ),
        name="score",
    )(activations, out_grads, basis_in, basis_out, eigenvalues, queries, doc_ids.reshape(1, tokens))
    return scores.T


def solution(mesh):
    wide, narrow = mesh.shape["wide"], mesh.shape["narrow"]

    def shards(activations, out_grads, basis_in, basis_out, eigenvalues, queries, doc_ids):
        return score(
            wide, narrow, activations, out_grads, basis_in, basis_out, eigenvalues, queries, doc_ids
        )

    return jax.shard_map(
        shards,
        mesh=mesh,
        in_specs=(
            P("wide", "narrow"),
            P("wide", None),
            P("narrow", "wide"),
            P("wide", "narrow"),
            P("narrow", "wide"),
            P(None, "narrow", "wide"),
            P(),
        ),
        out_specs=P(),
        check_vma=False,
    )
```

```python
import functools

import jax
import jax.numpy as jnp
from jax import lax
from jax.experimental import pallas as pl
from jax.experimental.pallas import tpu as pltpu
from jax.sharding import PartitionSpec as P

DOC_PER = 2
DAMPING = 0.1
F32 = jnp.float32
BF16 = jnp.bfloat16
ANY = pl.BlockSpec(memory_space=pl.ANY)
VMEM_LIMIT = 67_043_328


def tile_of(size, most):
    return max(t for t in range(128, most + 1, 128) if size % t == 0)


def grid_of(wide):
    outer = max(o for o in (1, 2, 3, 4) if wide % o == 0)
    return outer, wide // outer


def remote(src, dst, send, recv, device):
    return pltpu.make_async_remote_copy(
        src_ref=src,
        dst_ref=dst,
        send_sem=send,
        recv_sem=recv,
        device_id=device,
        device_id_type=pl.DeviceIdType.MESH,
    )


def greet(wide, narrow):
    w, n = lax.axis_index("wide"), lax.axis_index("narrow")
    barrier = pltpu.get_barrier_semaphore()
    for d in range(1, wide):
        pl.semaphore_signal(
            barrier, inc=1, device_id={"wide": lax.rem(w + d, wide)}, device_id_type=pl.DeviceIdType.MESH
        )
    for d in range(1, narrow):
        pl.semaphore_signal(
            barrier, inc=1, device_id={"narrow": lax.rem(n + d, narrow)}, device_id_type=pl.DeviceIdType.MESH
        )
    pl.semaphore_wait(barrier, wide + narrow - 2)


def score_kernel(
    wide, narrow, docs, acts, grads, basis_in, basis_out, eigenvalues, queries, ids, out,
    acts_all, weights, total, rows_held, weights_out, grads_part, grads_send, first_recv, second_send,
    second_recv, grads_all, acts_send, core_recv, cross_send, cross_recv, acts_done,
    eig_tile, query_tile, mixed, lanes, held, across,
    local_sem, weight_sem, out_sem, eig_sem, query_sem, a2a_s, a2a_r,
    line_s, line_r, side_s, side_r, gline_s, gline_r, gside_s, gside_r,
    first_s, first_r, second_s, second_r, core_s, core_r, cross_s, cross_r, done_s, done_r, last_s, last_r,
    send_w, recv_w, send_n, recv_n,
):
    outer, inner = grid_of(wide)
    cross = narrow // 2
    w, n = lax.axis_index("wide"), lax.axis_index("narrow")
    wo, wi = w // inner, lax.rem(w, inner)
    nx, nc = n // 2, lax.rem(n, 2)
    chunks, tokens, depth = acts_all.shape
    block = acts.shape[0]
    columns = total.shape[1]
    rows_out = basis_out.shape[0]
    half = tokens // 2

    def line_peer(d):
        return {"wide": lax.rem(wo + d, outer) * inner + wi}

    def side_peer(e):
        return {"wide": wo * inner + lax.rem(wi + e, inner)}

    def cut(c):
        return pl.ds(pl.multiple_of(c * depth, 128), depth)

    def rows(source):
        return pl.ds(pl.multiple_of(source * block, block), block)

    def line_source(d):
        return lax.rem(wo + outer - d, outer) * inner + wi

    def weight(c):
        slot = lax.rem(c, 2)
        return pltpu.make_async_copy(
            basis_in.at[pl.ds(pl.multiple_of(c * depth, 128), depth)], weights.at[slot], weight_sem.at[slot]
        )

    fetch_out = pltpu.make_async_copy(basis_out, weights_out, local_sem.at[0])
    own_rows = pltpu.make_async_copy(
        grads.at[:, pl.ds(pl.multiple_of(w * rows_out, 128), rows_out)], rows_held.at[rows(w)], local_sem.at[1]
    )

    def own_acts(c):
        return pltpu.make_async_copy(acts.at[:, cut(c)], acts_all.at[c, rows(w)], out_sem.at[c])

    own_rows.start()
    fetch_out.start()
    for c in range(chunks):
        own_acts(c).start()
    weight(0).start()
    weight(1).start()
    count, width, _ = queries.shape
    jt = eig_tile.shape[2]
    tiles = columns // jt

    def mix_columns(j):
        return pl.ds(pl.multiple_of(j * jt, 128), jt)

    def eig_copy(j):
        slot = lax.rem(j, 2)
        return pltpu.make_async_copy(eigenvalues.at[:, mix_columns(j)], eig_tile.at[slot], eig_sem.at[slot])

    def query_copy(j):
        slot = lax.rem(j, 2)
        return pltpu.make_async_copy(queries.at[:, :, mix_columns(j)], query_tile.at[slot], query_sem.at[slot])

    greet(wide, narrow)

    def swap(d):
        to = lax.rem(w + d, wide)
        return remote(
            grads.at[:, pl.ds(pl.multiple_of(to * rows_out, 128), rows_out)],
            rows_held.at[rows(w)],
            a2a_s.at[d],
            a2a_r.at[d],
            {"wide": to},
        )

    def line_copy(c, d):
        return remote(
            acts.at[:, cut(c)], acts_all.at[c, rows(w)], line_s.at[c, d], line_r.at[c, d], line_peer(d)
        )

    def side_own(c, e):
        return remote(
            acts.at[:, cut(c)], acts_all.at[c, rows(w)], side_s.at[c, e, 0], side_r.at[c, e, 0], side_peer(e)
        )

    def side_pass(c, e, d):
        source = line_source(d)
        return remote(
            acts_all.at[c, rows(source)],
            acts_all.at[c, rows(source)],
            side_s.at[c, e, d],
            side_r.at[c, e, d],
            side_peer(e),
        )

    def begin(c, carry):
        for d in range(1, outer):
            line_copy(c, d).start()
        for e in range(1, inner):
            side_own(c, e).start()
        return carry

    middle = chunks // 2
    for d in range(1, wide):
        swap(d).start()
    lax.fori_loop(0, middle + 1, begin, 0)
    wt = tile_of(width, 512)

    def grads_tile(k, carry):
        at = pl.ds(pl.multiple_of(k * wt, 128), wt)
        part = jnp.dot(rows_held[...], weights_out[:, at], preferred_element_type=F32)
        part = part.reshape(outer, inner, block, wt)
        grads_part[:, :, :, at] = part
        grads_send[:, :, :, at] = part.astype(BF16)
        return carry

    def first(e):
        return remote(
            grads_send.at[:, lax.rem(wi + e, inner)], first_recv.at[e], first_s.at[e], first_r.at[e], side_peer(e)
        )

    def second(d):
        return remote(
            second_send.at[lax.rem(wo + d, outer)], second_recv.at[d], second_s.at[d], second_r.at[d], line_peer(d)
        )

    ct = tile_of(columns, 512)

    def forward(c):
        for d in range(1, outer):
            line_copy(c, d).wait_recv()
            for e in range(1, inner):
                side_pass(c, e, d).start()

    def step(c, carry):
        @pl.when(c + 1 < chunks)
        def _():
            forward(c + 1)

        own_acts(c).wait()
        for e in range(1, inner):
            side_own(c, e).wait_recv()
            for d in range(1, outer):
                side_pass(c, e, d).wait_recv()
        weight(c).wait()
        slot = lax.rem(c, 2)

        def tile(k, carry):
            at = pl.ds(pl.multiple_of(k * ct, 128), ct)
            part = jnp.dot(acts_all[c], weights[slot, :, at], preferred_element_type=F32)

            @pl.when(c == 0)
            def _():
                total[:, at] = part

            @pl.when(c > 0)
            def _():
                total[:, at] += part

            return carry

        lax.fori_loop(0, columns // ct, tile, 0)

        @pl.when(c + 2 < chunks)
        def _():
            weight(c + 2).start()

        return carry

    own_rows.wait()
    fetch_out.wait()
    for d in range(1, wide):
        swap(d).wait_recv()
    lax.fori_loop(0, width // wt, grads_tile, 0)
    for e in range(1, inner):
        first(e).start()
    forward(0)
    lax.fori_loop(0, middle, step, 0)
    for e in range(1, inner):
        first(e).wait_recv()
    for o in range(outer):
        value = grads_part[o, wi]
        for e in range(1, inner):
            value = value + first_recv[e, o].astype(F32)
        second_send[o] = value
    for d in range(1, outer):
        second(d).start()
    lax.fori_loop(middle + 1, chunks, begin, 0)
    for j in range(2):
        eig_copy(j).start()
        query_copy(j).start()
    lax.fori_loop(middle, chunks, step, 0)

    share = half // cross

    def to_send(k, carry):
        at = pl.ds(pl.multiple_of(k * ct, 128), ct)
        acts_send[:, at] = total[pl.ds(pl.multiple_of((1 - nc) * half, half), half), at]
        return carry

    lax.fori_loop(0, columns // ct, to_send, 0)
    partner = {"narrow": nx * 2 + (1 - nc)}

    def cross_peer(d):
        return {"narrow": lax.rem(nx + d, cross) * 2 + nc}

    core_copy = remote(acts_send, core_recv, core_s, core_r, partner)
    core_copy.start()

    core_copy.wait_recv()

    def core_sum(k, carry):
        at = pl.ds(pl.multiple_of(k * ct, 128), ct)
        value = total[pl.ds(pl.multiple_of(nc * half, half), half), at] + core_recv[:, at]
        for x in range(cross):
            cross_send[x, :, at] = value[x * share : (x + 1) * share]
        return carry

    lax.fori_loop(0, columns // ct, core_sum, 0)

    def cross_copy(d):
        return remote(
            cross_send.at[lax.rem(nx + d, cross)], cross_recv.at[d], cross_s.at[d], cross_r.at[d], cross_peer(d)
        )

    for d in range(1, cross):
        cross_copy(d).start()

    for d in range(1, outer):
        second(d).wait_recv()
    value = second_send[wo]
    for d in range(1, outer):
        value = value + second_recv[d]
    grads_all[w] = value.astype(BF16)

    def gline(d):
        return remote(grads_all.at[w], grads_all.at[w], gline_s.at[d], gline_r.at[d], line_peer(d))

    def gside(e, d):
        source = line_source(d)
        return remote(
            grads_all.at[source], grads_all.at[source], gside_s.at[e, d], gside_r.at[e, d], side_peer(e)
        )

    for d in range(1, outer):
        gline(d).start()
    for e in range(1, inner):
        gside(e, 0).start()
    for d in range(1, outer):
        gline(d).wait_recv()
        for e in range(1, inner):
            gside(e, d).start()
    for e in range(1, inner):
        for d in range(outer):
            gside(e, d).wait_recv()

    def mix(j, carry):
        slot = lax.rem(j, 2)
        eig_copy(j).wait()
        query_copy(j).wait()
        left = grads_all[...].reshape(tokens, width)
        scale = 1.0 / (eig_tile[slot].astype(F32) + DAMPING)
        for q in range(count):
            precond = (query_tile[slot, q].astype(F32) * scale).astype(BF16)
            mixed[q, :, mix_columns(j)] = jnp.dot(left, precond, preferred_element_type=F32)

        @pl.when(j + 2 < tiles)
        def _():
            eig_copy(j + 2).start()
            query_copy(j + 2).start()

        return carry

    first_part = tiles // 4
    second_part = (3 * tiles) // 4
    lax.fori_loop(0, first_part, mix, 0)
    for d in range(1, cross):
        cross_copy(d).wait_recv()

    def cross_sum(k, carry):
        at = pl.ds(pl.multiple_of(k * ct, 128), ct)
        value = cross_send[nx, :, at]
        for d in range(1, cross):
            value = value + cross_recv[d, :, at]
        acts_done[nc, nx, :, at] = value.astype(BF16)
        return carry

    lax.fori_loop(0, columns // ct, cross_sum, 0)

    def done_copy(d):
        return remote(acts_done.at[nc, nx], acts_done.at[nc, nx], done_s.at[d], done_r.at[d], cross_peer(d))

    def last_copy(d):
        x = lax.rem(nx + cross - d, cross)
        return remote(acts_done.at[nc, x], acts_done.at[nc, x], last_s.at[d], last_r.at[d], partner)

    for d in range(1, cross):
        done_copy(d).start()
    last_copy(0).start()
    lax.fori_loop(first_part, second_part, mix, 0)
    for d in range(1, cross):
        done_copy(d).wait_recv()
        last_copy(d).start()
    lax.fori_loop(second_part, tiles, mix, 0)
    for d in range(cross):
        last_copy(d).wait_recv()

    lanes[...] = jnp.zeros_like(lanes)

    def fold(j, carry):
        at = pl.ds(pl.multiple_of(j * 128, 128), 128)
        right = acts_done[:, :, :, at].reshape(tokens, 128).astype(F32)
        for q in range(count):
            lanes[q] += mixed[q, :, at] * right
        return carry

    lax.fori_loop(0, columns // 128, fold, 0)
    _, rows_pad, docs_pad = across.shape
    member = (ids[...] == lax.broadcasted_iota(jnp.int32, (docs_pad, tokens), 0)).astype(F32)
    row = lax.broadcasted_iota(jnp.int32, (rows_pad, docs_pad), 0)
    value = jnp.zeros((rows_pad, docs_pad), F32)
    for q in range(count):
        doc_lanes = jnp.dot(member, lanes[q], precision=lax.Precision.HIGHEST, preferred_element_type=F32)
        value = jnp.where(row == q, jnp.sum(doc_lanes, axis=1)[None, :], value)
    across[n] = value

    def over_narrow(d):
        return remote(across.at[n], across.at[n], send_n.at[d], recv_n.at[d], {"narrow": lax.rem(n + d, narrow)})

    def over_wide(d):
        return remote(held.at[w], held.at[w], send_w.at[d], recv_w.at[d], {"wide": lax.rem(w + d, wide)})

    for d in range(1, narrow):
        over_narrow(d).start()
    for d in range(1, narrow):
        over_narrow(d).wait_recv()
    value = across[0]
    for d in range(1, narrow):
        value = value + across[d]
    held[w] = value
    for d in range(1, wide):
        over_wide(d).start()
    for d in range(1, wide):
        over_wide(d).wait_recv()
    value = held[0]
    for d in range(1, wide):
        value = value + held[d]
    out[...] = value[: out.shape[0], : out.shape[1]]

    for d in range(1, wide):
        swap(d).wait_send()

    def drain(c, carry):
        for d in range(1, outer):
            line_copy(c, d).wait_send()
        for e in range(1, inner):
            side_own(c, e).wait_send()
            for d in range(1, outer):
                side_pass(c, e, d).wait_send()
        return carry

    lax.fori_loop(0, chunks, drain, 0)
    for e in range(1, inner):
        first(e).wait_send()
        for d in range(outer):
            gside(e, d).wait_send()
    for d in range(1, outer):
        second(d).wait_send()
        gline(d).wait_send()
    core_copy.wait_send()
    for d in range(1, cross):
        cross_copy(d).wait_send()
        done_copy(d).wait_send()
    for d in range(cross):
        last_copy(d).wait_send()
    for d in range(1, narrow):
        over_narrow(d).wait_send()
    for d in range(1, wide):
        over_wide(d).wait_send()


def score(wide, narrow, activations, out_grads, basis_in, basis_out, eigenvalues, queries, doc_ids):
    outer, inner = grid_of(wide)
    cross = narrow // 2
    block, depth_all = activations.shape
    tokens = block * wide
    docs = DOC_PER * wide
    depth = tile_of(depth_all, 1024)
    chunks = depth_all // depth
    columns = basis_in.shape[1]
    rows_out, width = basis_out.shape
    count = queries.shape[0]
    half = tokens // 2
    jt = tile_of(columns, 256)
    rows_pad, docs_pad = pl.cdiv(count, 8) * 8, pl.cdiv(docs, 128) * 128
    dma = pltpu.SemaphoreType.DMA
    scores = pl.pallas_call(
        functools.partial(score_kernel, wide, narrow, docs),
        out_shape=jax.ShapeDtypeStruct((count, docs), F32),
        in_specs=[ANY] * 6 + [pl.BlockSpec(memory_space=pltpu.VMEM)],
        out_specs=pl.BlockSpec(memory_space=pltpu.VMEM),
        scratch_shapes=[
            pltpu.VMEM((chunks, tokens, depth), BF16),
            pltpu.VMEM((2, depth, columns), BF16),
            pltpu.VMEM((tokens, columns), F32),
            pltpu.VMEM((tokens, rows_out), BF16),
            pltpu.VMEM((rows_out, width), BF16),
            pltpu.VMEM((outer, inner, block, width), F32),
            pltpu.VMEM((outer, inner, block, width), BF16),
            pltpu.VMEM((inner, outer, block, width), BF16),
            pltpu.VMEM((outer, block, width), F32),
            pltpu.VMEM((outer, block, width), F32),
            pltpu.VMEM((wide, block, width), BF16),
            pltpu.VMEM((half, columns), F32),
            pltpu.VMEM((half, columns), F32),
            pltpu.VMEM((cross, half // cross, columns), F32),
            pltpu.VMEM((cross, half // cross, columns), F32),
            pltpu.VMEM((2, cross, half // cross, columns), BF16),
            pltpu.VMEM((2, width, jt), BF16),
            pltpu.VMEM((2, count, width, jt), BF16),
            pltpu.VMEM((count, tokens, columns), F32),
            pltpu.VMEM((count, tokens, 128), F32),
            pltpu.VMEM((wide, rows_pad, docs_pad), F32),
            pltpu.VMEM((narrow, rows_pad, docs_pad), F32),
            dma((2,)),
            dma((2,)),
            dma((chunks,)),
            dma((2,)),
            dma((2,)),
            dma((wide,)),
            dma((wide,)),
            dma((chunks, outer)),
            dma((chunks, outer)),
            dma((chunks, inner, outer)),
            dma((chunks, inner, outer)),
            dma((outer,)),
            dma((outer,)),
            dma((inner, outer)),
            dma((inner, outer)),
            dma((inner,)),
            dma((inner,)),
            dma((outer,)),
            dma((outer,)),
            dma,
            dma,
            dma((cross,)),
            dma((cross,)),
            dma((cross,)),
            dma((cross,)),
            dma((cross,)),
            dma((cross,)),
            dma((wide,)),
            dma((wide,)),
            dma((narrow,)),
            dma((narrow,)),
        ],
        compiler_params=pltpu.CompilerParams(
            collective_id=0, has_side_effects=True, vmem_limit_bytes=VMEM_LIMIT
        ),
        name="score",
    )(activations, out_grads, basis_in, basis_out, eigenvalues, queries, doc_ids.reshape(1, tokens))
    return scores.T


def solution(mesh):
    wide, narrow = mesh.shape["wide"], mesh.shape["narrow"]

    def shards(activations, out_grads, basis_in, basis_out, eigenvalues, queries, doc_ids):
        return score(
            wide, narrow, activations, out_grads, basis_in, basis_out, eigenvalues, queries, doc_ids
        )

    return jax.shard_map(
        shards,
        mesh=mesh,
        in_specs=(
            P("wide", "narrow"),
            P("wide", None),
            P("narrow", "wide"),
            P("wide", "narrow"),
            P("narrow", "wide"),
            P(None, "narrow", "wide"),
            P(),
        ),
        out_specs=P(),
        check_vma=False,
    )
```

```python
import functools

import jax
import jax.numpy as jnp
from jax import lax
from jax.experimental import pallas as pl
from jax.experimental.pallas import tpu as pltpu
from jax.sharding import PartitionSpec as P

DOC_PER = 2
DAMPING = 0.1
F32 = jnp.float32
BF16 = jnp.bfloat16
ANY = pl.BlockSpec(memory_space=pl.ANY)
VMEM_LIMIT = 67_043_328


def tile_of(size, most):
    return max(t for t in range(128, most + 1, 128) if size % t == 0)


def grid_of(wide):
    outer = max(o for o in (1, 2, 3, 4) if wide % o == 0)
    return outer, wide // outer


def remote(src, dst, send, recv, device):
    return pltpu.make_async_remote_copy(
        src_ref=src,
        dst_ref=dst,
        send_sem=send,
        recv_sem=recv,
        device_id=device,
        device_id_type=pl.DeviceIdType.MESH,
    )


def greet(wide, narrow):
    w, n = lax.axis_index("wide"), lax.axis_index("narrow")
    barrier = pltpu.get_barrier_semaphore()
    for d in range(1, wide):
        pl.semaphore_signal(
            barrier, inc=1, device_id={"wide": lax.rem(w + d, wide)}, device_id_type=pl.DeviceIdType.MESH
        )
    for d in range(1, narrow):
        pl.semaphore_signal(
            barrier, inc=1, device_id={"narrow": lax.rem(n + d, narrow)}, device_id_type=pl.DeviceIdType.MESH
        )
    pl.semaphore_wait(barrier, wide + narrow - 2)


def score_kernel(
    wide, narrow, docs, acts, grads, basis_in, basis_out, eigenvalues, queries, ids, out,
    acts_all, weights, total, rows_held, weights_out, grads_part, grads_send, first_recv, second_send,
    second_recv, grads_all, acts_send, core_recv, cross_send, cross_recv, acts_done,
    eig_tile, query_tile, mixed, lanes, held, across,
    local_sem, weight_sem, out_sem, eig_sem, query_sem, a2a_s, a2a_r,
    line_s, line_r, side_s, side_r, gline_s, gline_r, gside_s, gside_r,
    first_s, first_r, second_s, second_r, core_s, core_r, cross_s, cross_r, done_s, done_r, last_s, last_r,
    send_w, recv_w, send_n, recv_n,
):
    outer, inner = grid_of(wide)
    cross = narrow // 2
    w, n = lax.axis_index("wide"), lax.axis_index("narrow")
    wo, wi = w // inner, lax.rem(w, inner)
    nx, nc = n // 2, lax.rem(n, 2)
    chunks, tokens, depth = acts_all.shape
    block = acts.shape[0]
    columns = total.shape[1]
    rows_out = basis_out.shape[0]
    half = tokens // 2

    def line_peer(d):
        return {"wide": lax.rem(wo + d, outer) * inner + wi}

    def side_peer(e):
        return {"wide": wo * inner + lax.rem(wi + e, inner)}

    def cut(c):
        return pl.ds(pl.multiple_of(c * depth, 128), depth)

    def rows(source):
        return pl.ds(pl.multiple_of(source * block, block), block)

    def line_source(d):
        return lax.rem(wo + outer - d, outer) * inner + wi

    def weight(c):
        slot = lax.rem(c, 2)
        return pltpu.make_async_copy(
            basis_in.at[pl.ds(pl.multiple_of(c * depth, 128), depth)], weights.at[slot], weight_sem.at[slot]
        )

    fetch_out = pltpu.make_async_copy(basis_out, weights_out, local_sem.at[0])
    own_rows = pltpu.make_async_copy(
        grads.at[:, pl.ds(pl.multiple_of(w * rows_out, 128), rows_out)], rows_held.at[rows(w)], local_sem.at[1]
    )

    def own_acts(c):
        return pltpu.make_async_copy(acts.at[:, cut(c)], acts_all.at[c, rows(w)], out_sem.at[c])

    own_rows.start()
    fetch_out.start()
    for c in range(chunks):
        own_acts(c).start()
    weight(0).start()
    weight(1).start()
    count, width, _ = queries.shape
    jt = eig_tile.shape[2]
    tiles = columns // jt

    def mix_columns(j):
        return pl.ds(pl.multiple_of(j * jt, 128), jt)

    def eig_copy(j):
        slot = lax.rem(j, 2)
        return pltpu.make_async_copy(eigenvalues.at[:, mix_columns(j)], eig_tile.at[slot], eig_sem.at[slot])

    def query_copy(j):
        slot = lax.rem(j, 2)
        return pltpu.make_async_copy(queries.at[:, :, mix_columns(j)], query_tile.at[slot], query_sem.at[slot])

    greet(wide, narrow)

    def swap(d):
        to = lax.rem(w + d, wide)
        return remote(
            grads.at[:, pl.ds(pl.multiple_of(to * rows_out, 128), rows_out)],
            rows_held.at[rows(w)],
            a2a_s.at[d],
            a2a_r.at[d],
            {"wide": to},
        )

    def line_copy(c, d):
        return remote(
            acts.at[:, cut(c)], acts_all.at[c, rows(w)], line_s.at[c, d], line_r.at[c, d], line_peer(d)
        )

    def side_own(c, e):
        return remote(
            acts.at[:, cut(c)], acts_all.at[c, rows(w)], side_s.at[c, e, 0], side_r.at[c, e, 0], side_peer(e)
        )

    def side_pass(c, e, d):
        source = line_source(d)
        return remote(
            acts_all.at[c, rows(source)],
            acts_all.at[c, rows(source)],
            side_s.at[c, e, d],
            side_r.at[c, e, d],
            side_peer(e),
        )

    def begin(c, carry):
        for d in range(1, outer):
            line_copy(c, d).start()
        for e in range(1, inner):
            side_own(c, e).start()
        return carry

    middle = chunks // 2
    for d in range(1, wide):
        swap(d).start()
    lax.fori_loop(0, chunks, begin, 0)
    wt = tile_of(width, 512)

    def grads_tile(k, carry):
        at = pl.ds(pl.multiple_of(k * wt, 128), wt)
        part = jnp.dot(rows_held[...], weights_out[:, at], preferred_element_type=F32)
        part = part.reshape(outer, inner, block, wt)
        grads_part[:, :, :, at] = part
        grads_send[:, :, :, at] = part.astype(BF16)
        return carry

    def first(e):
        return remote(
            grads_send.at[:, lax.rem(wi + e, inner)], first_recv.at[e], first_s.at[e], first_r.at[e], side_peer(e)
        )

    def second(d):
        return remote(
            second_send.at[lax.rem(wo + d, outer)], second_recv.at[d], second_s.at[d], second_r.at[d], line_peer(d)
        )

    ct = tile_of(columns, 512)

    def forward(c):
        for d in range(1, outer):
            line_copy(c, d).wait_recv()
            for e in range(1, inner):
                side_pass(c, e, d).start()

    def step(c, carry):
        @pl.when(c + 1 < chunks)
        def _():
            forward(c + 1)

        own_acts(c).wait()
        for e in range(1, inner):
            side_own(c, e).wait_recv()
            for d in range(1, outer):
                side_pass(c, e, d).wait_recv()
        weight(c).wait()
        slot = lax.rem(c, 2)

        def tile(k, carry):
            at = pl.ds(pl.multiple_of(k * ct, 128), ct)
            part = jnp.dot(acts_all[c], weights[slot, :, at], preferred_element_type=F32)

            @pl.when(c == 0)
            def _():
                total[:, at] = part

            @pl.when(c > 0)
            def _():
                total[:, at] += part

            return carry

        lax.fori_loop(0, columns // ct, tile, 0)

        @pl.when(c + 2 < chunks)
        def _():
            weight(c + 2).start()

        return carry

    own_rows.wait()
    fetch_out.wait()
    for d in range(1, wide):
        swap(d).wait_recv()
    lax.fori_loop(0, width // wt, grads_tile, 0)
    for e in range(1, inner):
        first(e).start()
    forward(0)
    lax.fori_loop(0, middle, step, 0)
    for e in range(1, inner):
        first(e).wait_recv()
    for o in range(outer):
        value = grads_part[o, wi]
        for e in range(1, inner):
            value = value + first_recv[e, o].astype(F32)
        grads_part[o, wi] = value
        second_send[o] = value.astype(BF16)
    for d in range(1, outer):
        second(d).start()
    for j in range(2):
        eig_copy(j).start()
        query_copy(j).start()
    lax.fori_loop(middle, chunks, step, 0)

    share = half // cross

    def to_send(k, carry):
        at = pl.ds(pl.multiple_of(k * ct, 128), ct)
        acts_send[:, at] = total[pl.ds(pl.multiple_of((1 - nc) * half, half), half), at]
        return carry

    lax.fori_loop(0, columns // ct, to_send, 0)
    partner = {"narrow": nx * 2 + (1 - nc)}

    def cross_peer(d):
        return {"narrow": lax.rem(nx + d, cross) * 2 + nc}

    core_copy = remote(acts_send, core_recv, core_s, core_r, partner)
    core_copy.start()

    core_copy.wait_recv()

    def core_sum(k, carry):
        at = pl.ds(pl.multiple_of(k * ct, 128), ct)
        value = total[pl.ds(pl.multiple_of(nc * half, half), half), at] + core_recv[:, at]
        for x in range(cross):
            cross_send[x, :, at] = value[x * share : (x + 1) * share]
        return carry

    lax.fori_loop(0, columns // ct, core_sum, 0)

    def cross_copy(d):
        return remote(
            cross_send.at[lax.rem(nx + d, cross)], cross_recv.at[d], cross_s.at[d], cross_r.at[d], cross_peer(d)
        )

    for d in range(1, cross):
        cross_copy(d).start()

    for d in range(1, outer):
        second(d).wait_recv()
    value = grads_part[wo, wi]
    for d in range(1, outer):
        value = value + second_recv[d].astype(F32)
    grads_all[w] = value.astype(BF16)

    def gline(d):
        return remote(grads_all.at[w], grads_all.at[w], gline_s.at[d], gline_r.at[d], line_peer(d))

    def gside(e, d):
        source = line_source(d)
        return remote(
            grads_all.at[source], grads_all.at[source], gside_s.at[e, d], gside_r.at[e, d], side_peer(e)
        )

    for d in range(1, outer):
        gline(d).start()
    for e in range(1, inner):
        gside(e, 0).start()
    for d in range(1, outer):
        gline(d).wait_recv()
        for e in range(1, inner):
            gside(e, d).start()
    for e in range(1, inner):
        for d in range(outer):
            gside(e, d).wait_recv()

    def mix(j, carry):
        slot = lax.rem(j, 2)
        eig_copy(j).wait()
        query_copy(j).wait()
        left = grads_all[...].reshape(tokens, width)
        scale = 1.0 / (eig_tile[slot].astype(F32) + DAMPING)
        for q in range(count):
            precond = (query_tile[slot, q].astype(F32) * scale).astype(BF16)
            mixed[q, :, mix_columns(j)] = jnp.dot(left, precond, preferred_element_type=F32)

        @pl.when(j + 2 < tiles)
        def _():
            eig_copy(j + 2).start()
            query_copy(j + 2).start()

        return carry

    first_part = tiles // 4
    second_part = (3 * tiles) // 4
    lax.fori_loop(0, first_part, mix, 0)
    for d in range(1, cross):
        cross_copy(d).wait_recv()

    def cross_sum(k, carry):
        at = pl.ds(pl.multiple_of(k * ct, 128), ct)
        value = cross_send[nx, :, at]
        for d in range(1, cross):
            value = value + cross_recv[d, :, at]
        acts_done[nc, nx, :, at] = value.astype(BF16)
        return carry

    lax.fori_loop(0, columns // ct, cross_sum, 0)

    def done_copy(d):
        return remote(acts_done.at[nc, nx], acts_done.at[nc, nx], done_s.at[d], done_r.at[d], cross_peer(d))

    def last_copy(d):
        x = lax.rem(nx + cross - d, cross)
        return remote(acts_done.at[nc, x], acts_done.at[nc, x], last_s.at[d], last_r.at[d], partner)

    for d in range(1, cross):
        done_copy(d).start()
    last_copy(0).start()
    lax.fori_loop(first_part, second_part, mix, 0)
    for d in range(1, cross):
        done_copy(d).wait_recv()
        last_copy(d).start()
    lax.fori_loop(second_part, tiles, mix, 0)
    for d in range(cross):
        last_copy(d).wait_recv()

    lanes[...] = jnp.zeros_like(lanes)

    def fold(j, carry):
        at = pl.ds(pl.multiple_of(j * 128, 128), 128)
        right = acts_done[:, :, :, at].reshape(tokens, 128).astype(F32)
        for q in range(count):
            lanes[q] += mixed[q, :, at] * right
        return carry

    lax.fori_loop(0, columns // 128, fold, 0)
    _, rows_pad, docs_pad = across.shape
    member = (ids[...] == lax.broadcasted_iota(jnp.int32, (docs_pad, tokens), 0)).astype(F32)
    row = lax.broadcasted_iota(jnp.int32, (rows_pad, docs_pad), 0)
    value = jnp.zeros((rows_pad, docs_pad), F32)
    for q in range(count):
        doc_lanes = jnp.dot(member, lanes[q], precision=lax.Precision.HIGHEST, preferred_element_type=F32)
        value = jnp.where(row == q, jnp.sum(doc_lanes, axis=1)[None, :], value)
    across[n] = value

    def over_narrow(d):
        return remote(across.at[n], across.at[n], send_n.at[d], recv_n.at[d], {"narrow": lax.rem(n + d, narrow)})

    def over_wide(d):
        return remote(held.at[w], held.at[w], send_w.at[d], recv_w.at[d], {"wide": lax.rem(w + d, wide)})

    for d in range(1, narrow):
        over_narrow(d).start()
    for d in range(1, narrow):
        over_narrow(d).wait_recv()
    value = across[0]
    for d in range(1, narrow):
        value = value + across[d]
    held[w] = value
    for d in range(1, wide):
        over_wide(d).start()
    for d in range(1, wide):
        over_wide(d).wait_recv()
    value = held[0]
    for d in range(1, wide):
        value = value + held[d]
    out[...] = value[: out.shape[0], : out.shape[1]]

    for d in range(1, wide):
        swap(d).wait_send()

    def drain(c, carry):
        for d in range(1, outer):
            line_copy(c, d).wait_send()
        for e in range(1, inner):
            side_own(c, e).wait_send()
            for d in range(1, outer):
                side_pass(c, e, d).wait_send()
        return carry

    lax.fori_loop(0, chunks, drain, 0)
    for e in range(1, inner):
        first(e).wait_send()
        for d in range(outer):
            gside(e, d).wait_send()
    for d in range(1, outer):
        second(d).wait_send()
        gline(d).wait_send()
    core_copy.wait_send()
    for d in range(1, cross):
        cross_copy(d).wait_send()
        done_copy(d).wait_send()
    for d in range(cross):
        last_copy(d).wait_send()
    for d in range(1, narrow):
        over_narrow(d).wait_send()
    for d in range(1, wide):
        over_wide(d).wait_send()


def score(wide, narrow, activations, out_grads, basis_in, basis_out, eigenvalues, queries, doc_ids):
    outer, inner = grid_of(wide)
    cross = narrow // 2
    block, depth_all = activations.shape
    tokens = block * wide
    docs = DOC_PER * wide
    depth = tile_of(depth_all, 1024)
    chunks = depth_all // depth
    columns = basis_in.shape[1]
    rows_out, width = basis_out.shape
    count = queries.shape[0]
    half = tokens // 2
    jt = tile_of(columns, 256)
    rows_pad, docs_pad = pl.cdiv(count, 8) * 8, pl.cdiv(docs, 128) * 128
    dma = pltpu.SemaphoreType.DMA
    scores = pl.pallas_call(
        functools.partial(score_kernel, wide, narrow, docs),
        out_shape=jax.ShapeDtypeStruct((count, docs), F32),
        in_specs=[ANY] * 6 + [pl.BlockSpec(memory_space=pltpu.VMEM)],
        out_specs=pl.BlockSpec(memory_space=pltpu.VMEM),
        scratch_shapes=[
            pltpu.VMEM((chunks, tokens, depth), BF16),
            pltpu.VMEM((2, depth, columns), BF16),
            pltpu.VMEM((tokens, columns), F32),
            pltpu.VMEM((tokens, rows_out), BF16),
            pltpu.VMEM((rows_out, width), BF16),
            pltpu.VMEM((outer, inner, block, width), F32),
            pltpu.VMEM((outer, inner, block, width), BF16),
            pltpu.VMEM((inner, outer, block, width), BF16),
            pltpu.VMEM((outer, block, width), BF16),
            pltpu.VMEM((outer, block, width), BF16),
            pltpu.VMEM((wide, block, width), BF16),
            pltpu.VMEM((half, columns), F32),
            pltpu.VMEM((half, columns), F32),
            pltpu.VMEM((cross, half // cross, columns), F32),
            pltpu.VMEM((cross, half // cross, columns), F32),
            pltpu.VMEM((2, cross, half // cross, columns), BF16),
            pltpu.VMEM((2, width, jt), BF16),
            pltpu.VMEM((2, count, width, jt), BF16),
            pltpu.VMEM((count, tokens, columns), F32),
            pltpu.VMEM((count, tokens, 128), F32),
            pltpu.VMEM((wide, rows_pad, docs_pad), F32),
            pltpu.VMEM((narrow, rows_pad, docs_pad), F32),
            dma((2,)),
            dma((2,)),
            dma((chunks,)),
            dma((2,)),
            dma((2,)),
            dma((wide,)),
            dma((wide,)),
            dma((chunks, outer)),
            dma((chunks, outer)),
            dma((chunks, inner, outer)),
            dma((chunks, inner, outer)),
            dma((outer,)),
            dma((outer,)),
            dma((inner, outer)),
            dma((inner, outer)),
            dma((inner,)),
            dma((inner,)),
            dma((outer,)),
            dma((outer,)),
            dma,
            dma,
            dma((cross,)),
            dma((cross,)),
            dma((cross,)),
            dma((cross,)),
            dma((cross,)),
            dma((cross,)),
            dma((wide,)),
            dma((wide,)),
            dma((narrow,)),
            dma((narrow,)),
        ],
        compiler_params=pltpu.CompilerParams(
            collective_id=0, has_side_effects=True, vmem_limit_bytes=VMEM_LIMIT
        ),
        name="score",
    )(activations, out_grads, basis_in, basis_out, eigenvalues, queries, doc_ids.reshape(1, tokens))
    return scores.T


def solution(mesh):
    wide, narrow = mesh.shape["wide"], mesh.shape["narrow"]

    def shards(activations, out_grads, basis_in, basis_out, eigenvalues, queries, doc_ids):
        return score(
            wide, narrow, activations, out_grads, basis_in, basis_out, eigenvalues, queries, doc_ids
        )

    return jax.shard_map(
        shards,
        mesh=mesh,
        in_specs=(
            P("wide", "narrow"),
            P("wide", None),
            P("narrow", "wide"),
            P("wide", "narrow"),
            P("narrow", "wide"),
            P(None, "narrow", "wide"),
            P(),
        ),
        out_specs=P(),
        check_vma=False,
    )
```
